32 devices in a mesh: dp: 4 (over z), space: 8 (over y, x, core).
Axes of the slice: x: 2, y: 2, z: 4, core: 2. Of those that a mesh axis runs over, the one named last changes fastest.
Arguments:
- voxels: bfloat16 [16384, 256], P(('dp', 'space')), may hold values from -6 to 6
- counts: int32 [64], P(('dp', 'space')), may hold values from 32 to 256
- partners: int32 [64, 3], P(('dp', 'space')), may hold values from 0 to 63, as said below
- gain_attn: float32 [256], replicated, may hold values from 0.5 to 1.5
- w_qkv: bfloat16 [256, 768], replicated, may hold values from -5 to 5
- w_out: bfloat16 [256, 256], replicated, may hold values from -0.375 to 0.375
- gain_mlp: float32 [256], replicated, may hold values from 0.5 to 1.5
- w_up: bfloat16 [256, 1024], replicated, may hold values from -0.375 to 0.375
- w_down: bfloat16 [1024, 256], replicated, may hold values from -0.1875 to 0.1875
- cotangent: bfloat16 [16384, 256], P(('dp', 'space')), may hold values from -6 to 6
Outputs:
- output: bfloat16 [16384, 256], P(('dp', 'space'))
- grad_voxels: float32 [16384, 256], P(('dp', 'space'))
- grad_qkv: float32 [256, 768], replicated
- grad_out: float32 [256, 256], replicated
- grad_up: float32 [256, 1024], replicated
- grad_down: float32 [1024, 256], replicated
- grad_gain_attn: float32 [256], replicated
- grad_gain_mlp: float32 [256], replicated
The draws below stay inside these ranges and needn't reach their ends.
Inputs may be any that keep to these rules, and one draw needn't show every extreme that they name: `partners`: blocks are numbered so that each index of dp holds a contiguous range of 64 / 4 blocks. Row i lists blocks of the same range as block i, each within 2 blocks of i and never i itself.
All inputs are finite; a program needn't handle non-finite values.
Results may differ from the reference program's by a relative error of at most 0.024.
The reference program's roundings to bfloat16 on the way (of `normed`, `packed`, `attended`, `normed_mlp`, `hidden`, `grad_pre`, `grad_attended` and `grad_packed`) count: a program that leaves them out, or rounds other values in their place, can miss the bound.
Values may be sent and summed in bfloat16 or wider, within the bound.
A program may use at most 128 MiB of HBM per device.

```python
import math
import jax
import jax.numpy as jnp
from jax import lax

D = 256
HEADS = 8
HEAD = 32
FF = 1024
BS = 256
PART = 3
SPAN = 2
NBLOCKS = 64
TOKENS = 16384
N_DP = 4


def draw_partners(key, part):
    group_size = NBLOCKS // N_DP
    slots = jnp.arange(2 * SPAN, dtype=jnp.int32)
    table = jnp.where(slots < SPAN, slots - SPAN, slots - SPAN + 1)
    scores = jax.random.randint(key, (NBLOCKS, 2 * SPAN), 0, 1 << 20, dtype=jnp.int32) * (2 * SPAN) + slots[None, :]
    order = jnp.argsort(scores, axis=1)[:, :PART]
    offsets = jnp.take(table, order)
    block_ids = jnp.arange(NBLOCKS, dtype=jnp.int32)[:, None]
    inside = block_ids % group_size + offsets
    inside_ok = (inside >= 0) & (inside < group_size)
    offsets = jnp.where(inside_ok, offsets, -offsets)
    return (block_ids + offsets).astype(jnp.int32)


def draw_w_qkv(key, part):
    base = jax.random.truncated_normal(key, -3.0, 3.0, (D, 3 * D), jnp.float32) * D ** (-0.5)
    return base.astype(jnp.bfloat16)


def set_ends(result, rng, smallest, top_value):
    index_at = [jax.random.randint(jax.random.fold_in(rng, axis), (), 0, length) for axis, length in enumerate(result.shape)]
    longest = result.shape.index(max(result.shape))
    neighbour = index_at[:longest] + [(index_at[longest] + 1) % result.shape[longest]] + index_at[longest + 1:]
    return result.at[tuple(index_at)].set(smallest).at[tuple(neighbour)].set(top_value)


def steps_of(key, shape, pieces, low, largest):
    factor_of = 1.0
    for dim, parts in pieces:
        draws = jax.random.uniform(jax.random.fold_in(jax.random.fold_in(key, 6), dim), (parts,), jnp.float32, low / len(pieces), largest / len(pieces))
        factor_of = factor_of * jnp.repeat(jnp.exp(draws), shape[dim] // parts).reshape((-1,) + (1,) * (len(shape) - 1 - dim))
    return factor_of


def gaussian(key, dims, scale, bound, pieces=(), kind=jnp.bfloat16):
    gain = steps_of(key, dims, pieces, -0.22, 0.18) if pieces else 1.0
    drawn = jax.random.normal(key, dims, jnp.float32) * scale * gain
    return jnp.minimum(jnp.maximum(drawn, -bound), bound).astype(kind)


def setup_inputs(seed: int = 0) -> dict:
    key_list = jax.random.split(jax.random.key(seed), 11)
    voxels = gaussian(key_list[0], (TOKENS, D), 1.0, 6.0, ((0, 32),))
    counts = set_ends(jax.random.randint(key_list[1], (NBLOCKS,), BS // 8, BS + 1), jax.random.fold_in(key_list[1], 1), BS // 8, BS).astype(jnp.int32)
    partners = draw_partners(jax.random.fold_in(key_list[10], 71), 0)
    gain_attn = jnp.clip(1.0 + 0.1 * jax.random.normal(key_list[3], (D,), jnp.float32), 0.5, 1.5)
    w_qkv = draw_w_qkv(jax.random.fold_in(key_list[10], 71), 0)
    w_out = gaussian(key_list[5], (D, D), D ** -0.5, 0.375)
    gain_mlp = jnp.clip(1.0 + 0.1 * jax.random.normal(key_list[6], (D,), jnp.float32), 0.5, 1.5)
    w_up = gaussian(key_list[7], (D, FF), D ** -0.5, 0.375)
    w_down = gaussian(key_list[8], (FF, D), FF ** -0.5, 0.1875)
    cotangent = gaussian(key_list[9], (TOKENS, D), 1.0, 6.0, ((0, 32),))
    return dict(voxels=voxels, counts=counts, partners=partners, gain_attn=gain_attn, w_qkv=w_qkv, w_out=w_out, gain_mlp=gain_mlp, w_up=w_up, w_down=w_down, cotangent=cotangent)


epsilon = 1e-06
root_coef = math.sqrt(2.0 / math.pi)

def matmul(left, right):
    return jnp.dot(left, right, preferred_element_type=jnp.float32)

def outer_sum(left, right):
    return jnp.einsum('rd,re->de', left.astype(jnp.float32), right.astype(jnp.float32), precision=lax.Precision.HIGHEST)

def product(form, left, right):
    return jnp.einsum(form, left.astype(jnp.float32), right.astype(jnp.float32), precision=lax.Precision.HIGHEST)

def gelu_value(pre_act):
    tangent = jnp.tanh(root_coef * (pre_act + 0.044715 * pre_act * pre_act * pre_act))
    return 0.5 * pre_act * (1.0 + tangent)

def gelu_slope(pre_act):
    tangent = jnp.tanh(root_coef * (pre_act + 0.044715 * pre_act * pre_act * pre_act))
    return 0.5 * (1.0 + tangent) + 0.5 * pre_act * (1.0 - tangent * tangent) * root_coef * (1.0 + 3.0 * 0.044715 * pre_act * pre_act)

def norm_rows(row_values, gain_vec):
    inv_rms = lax.rsqrt(lax.optimization_barrier(jnp.mean(row_values * row_values, axis=-1, keepdims=True)) + epsilon)
    return (inv_rms, (row_values * inv_rms * gain_vec).astype(jnp.bfloat16))

def norm_back(row_values, inv_rms, gain_vec, grad_norm):
    scaled_grad = grad_norm * gain_vec
    grad_rows = inv_rms * (scaled_grad - row_values * inv_rms * inv_rms * lax.optimization_barrier(jnp.mean(scaled_grad * row_values, axis=-1, keepdims=True)))
    return (grad_rows, lax.optimization_barrier(jnp.sum(grad_norm * row_values * inv_rms, axis=0)))

def attend_weights(query, key_heads, key_valid):
    scores = product('qhd,khd->hqk', query, key_heads) / math.sqrt(query.shape[-1])
    scores = jnp.where(key_valid[None, None, :], scores, -1e+30)
    row_max = lax.optimization_barrier(jnp.max(scores, axis=-1, keepdims=True))
    expo = jnp.exp(scores - row_max)
    return expo / lax.optimization_barrier(jnp.sum(expo, axis=-1, keepdims=True))

def attend_forward(query, key_heads, value_heads, key_valid):
    weights = attend_weights(query, key_heads, key_valid).astype(jnp.bfloat16)
    return product('hqk,khd->qhd', weights, value_heads).astype(jnp.bfloat16)

def attend_backward(query, key_heads, value_heads, key_valid, grad_result):
    weights = attend_weights(query, key_heads, key_valid)
    weights_b = weights.astype(jnp.bfloat16)
    grad_values = product('hqk,qhd->khd', weights_b, grad_result)
    grad_w = product('qhd,khd->hqk', grad_result, value_heads)
    grad_scores = weights * (grad_w - lax.optimization_barrier(jnp.sum(weights * grad_w, axis=-1, keepdims=True))) / math.sqrt(query.shape[-1])
    grad_scores = grad_scores.astype(jnp.bfloat16)
    grad_query = product('hqk,khd->qhd', grad_scores, key_heads)
    grad_keys = product('hqk,qhd->khd', grad_scores, query)
    return (grad_query, grad_keys, grad_values)

def reference(voxels, counts, partners, gain_attn, w_qkv, w_out, gain_mlp, w_up, w_down, cotangent):
    row_values = voxels.astype(jnp.float32)
    inv_attn, normed = norm_rows(row_values, gain_attn)
    packed = matmul(normed, w_qkv).astype(jnp.bfloat16)
    blocks = packed.reshape(NBLOCKS, BS, 3 * D)
    query_blocks = blocks[:, :, :D].reshape(NBLOCKS, BS, HEADS, HEAD)
    pair_blocks = blocks[:, :, D:]
    chosen = jnp.concatenate([jnp.arange(NBLOCKS, dtype=jnp.int32)[:, None], partners.astype(jnp.int32)], axis=1)
    position = jnp.arange(BS, dtype=jnp.int32)

    def keys_of(block_index):
        picked = jnp.take(pair_blocks, chosen[block_index], axis=0)
        key_valid = (position[None, :] < jnp.take(counts, chosen[block_index])[:, None]).reshape(-1)
        key_heads = picked[:, :, :D].reshape((PART + 1) * BS, HEADS, HEAD)
        value_heads = picked[:, :, D:].reshape((PART + 1) * BS, HEADS, HEAD)
        return (key_heads, value_heads, key_valid)

    def forward_block(block_index):
        key_heads, value_heads, key_valid = keys_of(block_index)
        return attend_forward(query_blocks[block_index], key_heads, value_heads, key_valid)
    attended = lax.map(forward_block, jnp.arange(NBLOCKS, dtype=jnp.int32)).reshape(TOKENS, D)
    mixed = row_values + matmul(attended, w_out)
    inv_mlp, normed_mlp = norm_rows(mixed, gain_mlp)
    pre_act = matmul(normed_mlp, w_up)
    hidden = gelu_value(pre_act).astype(jnp.bfloat16)
    output = (mixed + matmul(hidden, w_down)).astype(jnp.bfloat16)
    upstream = cotangent.astype(jnp.float32)
    down_sum = outer_sum(hidden, cotangent)
    grad_pre = (matmul(cotangent, w_down.T) * gelu_slope(pre_act)).astype(jnp.bfloat16)
    up_sum = outer_sum(normed_mlp, grad_pre)
    grad_normed_mlp = matmul(grad_pre, w_up.T)
    grad_through, gain_mlp_sum = norm_back(mixed, inv_mlp, gain_mlp, grad_normed_mlp)
    grad_mixed = upstream + grad_through
    grad_mixed_b = grad_mixed.astype(jnp.bfloat16)
    out_sum = outer_sum(attended, grad_mixed_b)
    grad_attended = matmul(grad_mixed_b, w_out.T).astype(jnp.bfloat16).reshape(NBLOCKS, BS, HEADS, HEAD)

    def backward_block(grad_acc, block_index):
        key_heads, value_heads, key_valid = keys_of(block_index)
        grad_query, grad_keys, grad_values = attend_backward(query_blocks[block_index], key_heads, value_heads, key_valid, grad_attended[block_index])
        stacked = jnp.concatenate([grad_keys.reshape(PART + 1, BS, D), grad_values.reshape(PART + 1, BS, D)], axis=-1)
        for member in range(PART + 1):
            grad_acc = grad_acc.at[chosen[block_index, member]].add(stacked[member])
        return (grad_acc, grad_query)
    grad_pairs, grad_queries = lax.scan(backward_block, jnp.zeros((NBLOCKS, BS, 2 * D), jnp.float32), jnp.arange(NBLOCKS, dtype=jnp.int32))
    grad_packed = jnp.concatenate([grad_queries.reshape(TOKENS, D), grad_pairs.reshape(TOKENS, 2 * D)], axis=-1).astype(jnp.bfloat16)
    qkv_sum = outer_sum(normed, grad_packed)
    grad_normed = matmul(grad_packed, w_qkv.T)
    grad_rows, gain_attn_sum = norm_back(row_values, inv_attn, gain_attn, grad_normed)
    grad_voxels = grad_mixed + grad_rows
    factor = 1.0 / math.sqrt(TOKENS)
    return (output, grad_voxels, qkv_sum * factor, out_sum * factor, up_sum * factor, down_sum * factor, gain_attn_sum * factor, gain_mlp_sum * factor)
```

```python
import functools
import math

import jax
import jax.numpy as jnp
from jax import lax
from jax.experimental import pallas as pl
from jax.experimental.pallas import tpu as pltpu
from jax.sharding import PartitionSpec as P

HEADS = 8
HEAD = 32
BS = 256
PART = 3
SPAN = 2


epsilon = 1e-06
root_coef = math.sqrt(2.0 / math.pi)


def padded(x, sides, width):
    for axis, dim in sides:
        devices, length = (lax.axis_size(axis), x.shape[dim])
        up = [(i, (i + 1) % devices) for i in range(devices - 1)]
        down = [(j, i) for i, j in up]
        last = lax.slice_in_dim(x, length - width, length, axis=dim)
        first = lax.slice_in_dim(x, 0, width, axis=dim)
        before = lax.ppermute(last, axis, up)
        after = lax.ppermute(first, axis, down)
        x = jnp.concatenate([before, x, after], axis=dim)
    return x


def from_behind(x, axis, by):
    devices = lax.axis_size(axis)
    pairs = [(i, i + by) for i in range(devices) if 0 <= i + by < devices]
    return lax.ppermute(x, axis, pairs)


def matmul(left, right):
    return jnp.dot(left, right, preferred_element_type=jnp.float32)


def times_transpose(left, right):
    return lax.dot_general(
        left, right, (((1,), (1,)), ((), ())), preferred_element_type=jnp.float32
    )


def outer_sum(left, right):
    return lax.dot_general(
        left, right, (((0,), (0,)), ((), ())), preferred_element_type=jnp.float32
    )


def norm_rows(row_values, gain_vec):
    inv_rms = lax.rsqrt(jnp.mean(row_values * row_values, axis=-1, keepdims=True) + epsilon)
    return (inv_rms, (row_values * inv_rms * gain_vec).astype(jnp.bfloat16))


def norm_back(row_values, inv_rms, gain_vec, grad_norm):
    scaled_grad = grad_norm * gain_vec
    grad_rows = inv_rms * (
        scaled_grad
        - row_values
        * inv_rms
        * inv_rms
        * jnp.mean(scaled_grad * row_values, axis=-1, keepdims=True)
    )
    return (grad_rows, jnp.sum(grad_norm * row_values * inv_rms, axis=0))


def head_mask(shape, axis, head):
    return lax.broadcasted_iota(jnp.int32, shape, axis) // HEAD == head


def layer_kernel(
    chosen, counts, xe, cot, gain_a, wqkv, wout, gain_m, wup, wdown,
    out_ref, gmix_ref, dq_ref, gext_ref, down_ref, up_ref, outsum_ref, gsum_ref,
    k_s, v_s, kt_s, vt_s, q_s, ksel, vsel, tsel, bias, wt, dst, att_t, gat_s, ga_s,
    mixed_s, nm_s, acc1, acc2, bd,
):
    d = wout.shape[0]
    ne = xe.shape[0] // BS
    nb = cot.shape[0] // BS
    members = PART + 1
    ff = wup.shape[1]
    scale = 1.0 / math.sqrt(HEAD)
    bf = jnp.bfloat16

    def project(e, c):
        rows = pl.ds(pl.multiple_of(e * BS, BS), BS)
        _, normed = norm_rows(xe[rows, :].astype(jnp.float32), gain_a[...])
        pair = matmul(normed, wqkv[:, d:])
        k, v = pair[:, :d].astype(bf), pair[:, d:].astype(bf)
        k_s[e], v_s[e] = k, v
        kt_s[e], vt_s[e] = k.T, v.T
        return c

    lax.fori_loop(0, ne, project, 0)

    def project_q(b, c):
        rows = pl.ds(pl.multiple_of((b + SPAN) * BS, BS), BS)
        _, normed = norm_rows(xe[rows, :].astype(jnp.float32), gain_a[...])
        q_s[b] = matmul(normed, wqkv[:, :d]).astype(bf)
        return c

    lax.fori_loop(0, nb, project_q, 0)

    def forward(b, c):
        for m in range(members):
            e = chosen[b, m]
            ksel[m * BS : (m + 1) * BS, :] = k_s[e]
            tsel[:, m * BS : (m + 1) * BS] = vt_s[e]
            slot = lax.broadcasted_iota(jnp.int32, (BS, BS), 0)
            bias[m * BS : (m + 1) * BS, :] = jnp.where(slot < counts[e], 0.0, -1e30)
        bd[0] = q_s[b].T

        def head(h, c):
            qm = jnp.where(head_mask((d, BS), 0, h), bd[0], 0)
            s = matmul(ksel[...], qm) + bias[...]
            top = jnp.max(s, axis=0, keepdims=True)
            e = jnp.exp((s - top) * scale)
            w = (e * (1.0 / jnp.sum(e, axis=0, keepdims=True))).astype(bf)
            lanes = pl.ds(pl.multiple_of(h * BS, BS), BS)
            wt[b, :, lanes] = w
            rows = pl.ds(pl.multiple_of(h * HEAD, HEAD), HEAD)
            att_t[b, rows, :] = matmul(tsel[rows, :], w)
            return c

        lax.fori_loop(0, HEADS, head, 0)
        rows = pl.ds(pl.multiple_of(b * BS, BS), BS)
        att = att_t[b].T.astype(bf)
        ga_s[rows, :] = att
        own = pl.ds(pl.multiple_of((b + SPAN) * BS, BS), BS)
        mixed = xe[own, :].astype(jnp.float32) + matmul(att, wout[...])
        mixed_s[rows, :] = mixed
        nm_s[rows, :] = norm_rows(mixed, gain_m[...])[1]
        return c

    lax.fori_loop(0, nb, forward, 0)

    acc1[...] = jnp.zeros_like(acc1)
    acc2[...] = jnp.zeros_like(acc2)

    def mlp(j, c):
        lanes = pl.ds(pl.multiple_of(j * BS, BS), BS)
        up, down = wup[:, lanes], wdown[lanes, :]
        pre = matmul(nm_s[...], up)
        sq = pre * pre
        tangent = jnp.tanh(root_coef * (pre + 0.044715 * sq * pre))
        half = 0.5 * (1.0 + tangent)
        hidden = (pre * half).astype(bf)
        slope = half + 0.5 * pre * (1.0 - tangent * tangent) * root_coef * (
            1.0 + 3.0 * 0.044715 * sq
        )
        acc1[...] += matmul(hidden, down)
        down_ref[lanes, :] = outer_sum(hidden, cot[...]).astype(bf)
        grad_pre = (times_transpose(cot[...], down) * slope).astype(bf)
        up_ref[lanes, :] = outer_sum(nm_s[...], grad_pre).astype(bf)
        acc2[...] += times_transpose(grad_pre, up)
        return c

    lax.fori_loop(0, ff // BS, mlp, 0)

    mixed = mixed_s[...]
    out_ref[...] = (mixed + acc1[...]).astype(bf)
    inv = lax.rsqrt(jnp.mean(mixed * mixed, axis=-1, keepdims=True) + epsilon)
    through, gsum = norm_back(mixed, inv, gain_m[...], acc2[...])
    gsum_ref[...] = jnp.broadcast_to(gsum[None, :], gsum_ref.shape)
    gmix = cot[...].astype(jnp.float32) + through
    gmix_ref[...] = gmix
    gb = gmix.astype(bf)
    outsum_ref[...] = outer_sum(ga_s[...], gb).astype(bf)
    ga = times_transpose(gb, wout[...]).astype(bf)
    ga_s[...] = ga
    for b in range(nb):
        gat_s[b] = ga[b * BS : (b + 1) * BS, :].T
    gext_ref[...] = jnp.zeros_like(gext_ref)

    def backward(b, c):
        for m in range(members):
            e = chosen[b, m]
            vsel[m * BS : (m + 1) * BS, :] = v_s[e]
            tsel[:, m * BS : (m + 1) * BS] = kt_s[e]

        def head(h, c):
            gm = jnp.where(head_mask((d, BS), 0, h), gat_s[b], 0)
            rows = pl.ds(pl.multiple_of(h * HEAD, HEAD), HEAD)
            lanes = pl.ds(pl.multiple_of(h * BS, BS), BS)
            delta = jnp.sum(
                att_t[b, rows, :] * gat_s[b, rows, :].astype(jnp.float32), axis=0, keepdims=True
            )
            gw = matmul(vsel[...], gm)
            ds = (wt[b, :, lanes].astype(jnp.float32) * (gw - delta)).astype(bf)
            dst[:, lanes] = ds
            att_t[b, rows, :] = matmul(tsel[rows, :], ds) * scale
            return c

        lax.fori_loop(0, HEADS, head, 0)
        rows = pl.ds(pl.multiple_of(b * BS, BS), BS)
        dq_ref[rows, :] = att_t[b].T.astype(bf)
        for h in range(HEADS):
            mask = head_mask((BS, d), 1, h)
            bd[h] = jnp.where(mask, q_s[b], 0)
        q_bd = bd[...].reshape(HEADS * BS, d)
        for m in range(members):
            dk = matmul(dst[m * BS : (m + 1) * BS, :], q_bd) * scale
            gext_ref[chosen[b, m], :, :d] += dk
        for h in range(HEADS):
            mask = head_mask((BS, d), 1, h)
            bd[h] = jnp.where(mask, ga_s[rows, :], 0)
        g_bd = bd[...].reshape(HEADS * BS, d)
        for m in range(members):
            dv = matmul(wt[b, m * BS : (m + 1) * BS, :], g_bd)
            gext_ref[chosen[b, m], :, d:] += dv
        return c

    lax.fori_loop(0, nb, backward, 0)


def layer(chosen, counts, xe, cot, gain_a, wqkv, wout, gain_m, wup, wdown):
    d = wout.shape[0]
    rows = cot.shape[0]
    nb, ne = rows // BS, xe.shape[0] // BS
    keys = (PART + 1) * BS
    ff = wup.shape[1]
    bf, f32 = jnp.bfloat16, jnp.float32
    vmem = pl.BlockSpec(memory_space=pltpu.VMEM)
    smem = pl.BlockSpec(memory_space=pltpu.SMEM)
    shape = jax.ShapeDtypeStruct
    return pl.pallas_call(
        layer_kernel,
        out_shape=[
            shape((rows, d), bf),
            shape((rows, d), f32),
            shape((rows, d), bf),
            shape((ne, BS, 2 * d), f32),
            shape((ff, d), bf),
            shape((ff, d), bf),
            shape((d, d), bf),
            shape((8, d), f32),
        ],
        in_specs=[smem, smem] + [vmem] * 8,
        out_specs=[vmem] * 8,
        scratch_shapes=[
            pltpu.VMEM((ne, BS, d), bf),
            pltpu.VMEM((ne, BS, d), bf),
            pltpu.VMEM((ne, d, BS), bf),
            pltpu.VMEM((ne, d, BS), bf),
            pltpu.VMEM((nb, BS, d), bf),
            pltpu.VMEM((keys, d), bf),
            pltpu.VMEM((keys, d), bf),
            pltpu.VMEM((d, keys), bf),
            pltpu.VMEM((keys, BS), f32),
            pltpu.VMEM((nb, keys, HEADS * BS), bf),
            pltpu.VMEM((keys, HEADS * BS), bf),
            pltpu.VMEM((nb, d, BS), f32),
            pltpu.VMEM((nb, d, BS), bf),
            pltpu.VMEM((rows, d), bf),
            pltpu.VMEM((rows, d), f32),
            pltpu.VMEM((rows, d), bf),
            pltpu.VMEM((rows, d), f32),
            pltpu.VMEM((rows, d), f32),
            pltpu.VMEM((HEADS, BS, d), bf),
        ],
        compiler_params=pltpu.CompilerParams(vmem_limit_bytes=60 << 20),
        name="layer",
    )(chosen, counts, xe, cot, gain_a.reshape(1, d), wqkv, wout, gain_m.reshape(1, d), wup, wdown)


def stage_list(sizes):
    stages = []
    for axis, size in sizes:
        bit = 1
        while bit < size:
            stages.append((axis, bit))
            bit *= 2
    return stages


def flip(axis, bit):
    me = lax.axis_index(axis)
    high = (me // bit) % 2
    return high, me + bit - 2 * bit * high


def sum_kernel(stages, g0, g1, g2, gains, r0, r1, r2, gains_out, work, land, gwork, gland, send, recv):
    parts, results = (g0, g1, g2), (r0, r1, r2)
    count = len(stages)
    rest = stages[1:]
    orders = []
    for p in range(3):
        turn = p % max(len(rest), 1)
        orders.append(stages[:1] + rest[turn:] + rest[:turn])
    barrier = pltpu.get_barrier_semaphore()
    for axis, bit in stages:
        pl.semaphore_signal(barrier, inc=1, device_id={axis: flip(axis, bit)[1]})
    pl.semaphore_wait(barrier, count)

    def remote(src, dst, p, s, axis, partner):
        copy = pltpu.make_async_remote_copy(
            src_ref=src, dst_ref=dst, send_sem=send.at[p, s], recv_sem=recv.at[p, s],
            device_id={axis: partner},
        )
        copy.start()
        return copy

    rows = g0.shape[0]
    size, start, landing = [rows] * 3, [0] * 3, [0] * 3
    history = [[], [], []]
    gwork[0] = gains[...]
    for s in range(count):
        pending = []
        for p in range(3):
            axis, bit = orders[p][s]
            high, partner = flip(axis, bit)
            source = parts[p] if s == 0 else work.at[p]
            half = size[p] // 2
            if half % 16 == 0:
                keep = pl.multiple_of(start[p] + high * half, 16)
                give = pl.multiple_of(start[p] + (1 - high) * half, 16)
                history[p].append((axis, partner, keep, half))
            else:
                half = size[p]
                keep = give = start[p]
            dst = land.at[p, pl.ds(landing[p], half)]
            pending.append((remote(source.at[pl.ds(give, half)], dst, p, s, axis, partner), source, keep, half))
        axis, bit = stages[s]
        extra = remote(gwork.at[s], gland.at[s], 3, s, axis, flip(axis, bit)[1])
        for p in range(3):
            copy, source, keep, half = pending[p]
            copy.wait()
            here = source[pl.ds(keep, half), :].astype(jnp.float32)
            there = land[p, landing[p] : landing[p] + half, :].astype(jnp.float32)
            total = (here + there).astype(jnp.bfloat16)
            target = results[p] if s == count - 1 else work.at[p]
            target[pl.ds(keep, half), :] = total
            start[p], size[p] = keep, half
            landing[p] += half
        extra.wait()
        gwork[s + 1] = gwork[s] + gland[s]
    gains_out[...] = gwork[count]
    deepest = max(len(h) for h in history)
    for s in range(deepest):
        pending = []
        for p in range(3):
            axis, partner, keep, half = history[p][len(history[p]) - 1 - s]
            region = results[p].at[pl.ds(keep, half)]
            pending.append(remote(region, region, p, count + s, axis, partner))
        for copy in pending:
            copy.wait()


def sum_all(g0, g1, g2, gains):
    sizes = [(axis, lax.axis_size(axis)) for axis in ("space", "dp")]
    stages = stage_list(sizes)
    count = len(stages)
    rows, d = g0.shape
    bf, f32 = jnp.bfloat16, jnp.float32
    vmem = pl.BlockSpec(memory_space=pltpu.VMEM)
    shape = jax.ShapeDtypeStruct
    return pl.pallas_call(
        functools.partial(sum_kernel, stages),
        out_shape=[shape((rows, d), bf)] * 3 + [shape(gains.shape, f32)],
        in_specs=[vmem] * 4,
        out_specs=[vmem] * 4,
        scratch_shapes=[
            pltpu.VMEM((3, rows, d), bf),
            pltpu.VMEM((3, rows + 16 * count, d), bf),
            pltpu.VMEM((count + 1,) + gains.shape, f32),
            pltpu.VMEM((count,) + gains.shape, f32),
            pltpu.SemaphoreType.DMA((4, 2 * count)),
            pltpu.SemaphoreType.DMA((4, 2 * count)),
        ],
        compiler_params=pltpu.CompilerParams(collective_id=0, has_side_effects=True),
        name="sum_all",
    )(g0, g1, g2, gains)


def body(voxels, counts, partners, gain_attn, w_qkv, w_out, gain_mlp, w_up, w_down, cotangent):
    model_width = w_out.shape[0]
    local_blocks = counts.shape[0]
    local_rows = voxels.shape[0]
    first_block = (
        lax.axis_index("dp") * lax.axis_size("space") + lax.axis_index("space")
    ) * local_blocks
    x_ext = padded(voxels, (("space", 0),), SPAN * BS)
    counts_ext = padded(counts, (("space", 0),), SPAN)
    own_ids = jnp.arange(local_blocks, dtype=jnp.int32)[:, None] + first_block
    chosen = jnp.concatenate([own_ids, partners], axis=1) - first_block + SPAN
    output, grad_mixed, grad_q, grad_ext, down_sum, up_sum, out_sum, gain_mlp_sum = layer(
        chosen, counts_ext, x_ext, cotangent, gain_attn, w_qkv, w_out, gain_mlp, w_up, w_down
    )
    from_lower = from_behind(grad_ext[local_blocks + SPAN :].astype(jnp.bfloat16), "space", 1)
    from_upper = from_behind(grad_ext[:SPAN].astype(jnp.bfloat16), "space", -1)
    grad_pairs = grad_ext[SPAN : SPAN + local_blocks]
    grad_pairs = grad_pairs.at[:SPAN].add(from_lower.astype(jnp.float32))
    grad_pairs = grad_pairs.at[local_blocks - SPAN :].add(from_upper.astype(jnp.float32))
    grad_packed = jnp.concatenate(
        [grad_q, grad_pairs.reshape(local_rows, 2 * model_width).astype(jnp.bfloat16)], axis=-1
    )
    row_values = voxels.astype(jnp.float32)
    inv_attn, normed = norm_rows(row_values, gain_attn)
    qkv_sum = outer_sum(grad_packed, normed).astype(jnp.bfloat16)
    grad_normed = times_transpose(grad_packed, w_qkv)
    grad_rows, gain_attn_sum = norm_back(row_values, inv_attn, gain_attn, grad_normed)
    grad_voxels = grad_mixed + grad_rows
    last = jnp.concatenate([out_sum, qkv_sum], axis=0)
    gains = jnp.concatenate([gain_attn_sum[None], gain_mlp_sum[:7]], axis=0)
    down, up, rest, gains = sum_all(down_sum, up_sum, last, gains)
    factor = 1.0 / math.sqrt(local_rows * lax.axis_size("dp") * lax.axis_size("space"))

    def scaled(value):
        return value.astype(jnp.float32) * factor

    grad_up = scaled(up).reshape(-1, model_width, BS).transpose(1, 0, 2).reshape(model_width, -1)
    return (
        output,
        grad_voxels,
        scaled(rest[model_width:]).T,
        scaled(rest[:model_width]),
        grad_up,
        scaled(down),
        scaled(gains[0]),
        scaled(gains[1]),
    )


def solution(mesh):
    in_specs = (
        P(("dp", "space"), None),
        P(("dp", "space")),
        P(("dp", "space"), None),
        P(),
        P(),
        P(),
        P(),
        P(),
        P(),
        P(("dp", "space"), None),
    )
    out_specs = (P(("dp", "space"), None), P(("dp", "space"), None), P(), P(), P(), P(), P(), P())
    return jax.shard_map(body, mesh=mesh, in_specs=in_specs, out_specs=out_specs, check_vma=False)
```

```python
import functools
import math

import jax
import jax.numpy as jnp
from jax import lax
from jax.experimental import pallas as pl
from jax.experimental.pallas import tpu as pltpu
from jax.sharding import PartitionSpec as P

HEADS = 8
HEAD = 32
BS = 256
PART = 3
SPAN = 2


epsilon = 1e-06
root_coef = math.sqrt(2.0 / math.pi)


def matmul(left, right):
    return jnp.dot(left, right, preferred_element_type=jnp.float32)


def times_transpose(left, right):
    return lax.dot_general(
        left, right, (((1,), (1,)), ((), ())), preferred_element_type=jnp.float32
    )


def outer_sum(left, right):
    return lax.dot_general(
        left, right, (((0,), (0,)), ((), ())), preferred_element_type=jnp.float32
    )


def norm_rows(row_values, gain_vec):
    inv_rms = lax.rsqrt(jnp.mean(row_values * row_values, axis=-1, keepdims=True) + epsilon)
    return (inv_rms, (row_values * inv_rms * gain_vec).astype(jnp.bfloat16))


def norm_back(row_values, inv_rms, gain_vec, grad_norm):
    scaled_grad = grad_norm * gain_vec
    grad_rows = inv_rms * (
        scaled_grad
        - row_values
        * inv_rms
        * inv_rms
        * jnp.mean(scaled_grad * row_values, axis=-1, keepdims=True)
    )
    return (grad_rows, jnp.sum(grad_norm * row_values * inv_rms, axis=0))


def head_mask(shape, axis, head):
    return lax.broadcasted_iota(jnp.int32, shape, axis) // HEAD == head


def stage_list(sizes):
    stages = []
    for axis, size in sizes:
        bit = 1
        while bit < size:
            stages.append((axis, bit))
            bit *= 2
    return stages


def flip(axis, bit):
    me = lax.axis_index(axis)
    high = (me // bit) % 2
    return high, me + bit - 2 * bit * high


def layer_kernel(
    stages, sizes_sd, x_in, cnt_in, partners, gain_a, wqkv, wout, gain_m, wup, wdown, cot,
    out_ref, gvox_ref, gqkv_ref, gout_ref, gup_ref, gdown_ref, ggain_a_ref, ggain_m_ref,
    xe, cnt, nrm_s, k_s, v_s, kt_s, vt_s, q_s, ksel, vsel, tsel, bias, wt, dst, att_t, gat_s,
    ga_s, mixed_s, nm_s, acc1, acc2, bd, dq_s, gext, gsend, gland,
    src0, src1, src2, src3, work0, work1, work2, work3, land0, land1, land2, land3,
    res0, res1, res2, res3, gwork, gainland, send, recv, hsend, hrecv,
):
    d = wout.shape[0]
    rows = cot.shape[0]
    nb = rows // BS
    ne = nb + 2 * SPAN
    members = PART + 1
    ff = wup.shape[1]
    scale = 1.0 / math.sqrt(HEAD)
    bf, f32 = jnp.bfloat16, jnp.float32
    space, dp = sizes_sd
    me = lax.axis_index("space")
    first = (lax.axis_index("dp") * space + me) * nb
    below, above = (me + space - 1) % space, (me + 1) % space
    count = len(stages)
    halo = SPAN * BS
    factor = 1.0 / math.sqrt(rows * space * dp)

    barrier = pltpu.get_barrier_semaphore()
    for axis, bit in stages:
        pl.semaphore_signal(barrier, inc=1, device_id={axis: flip(axis, bit)[1]})
    pl.semaphore_signal(barrier, inc=1, device_id={"space": below})
    pl.semaphore_signal(barrier, inc=1, device_id={"space": above})
    pl.semaphore_wait(barrier, count + 2)

    def shift(src, dst, slot, target):
        copy = pltpu.make_async_remote_copy(
            src_ref=src, dst_ref=dst, send_sem=hsend.at[slot], recv_sem=hrecv.at[slot],
            device_id={"space": target},
        )
        copy.start()
        return copy

    halos = [
        shift(x_in.at[pl.ds(0, halo)], xe.at[pl.ds((nb + SPAN) * BS, halo)], 0, below),
        shift(x_in.at[pl.ds(rows - halo, halo)], xe.at[pl.ds(0, halo)], 1, above),
        shift(cnt_in.at[pl.ds(0, SPAN)], cnt.at[pl.ds(nb + SPAN, SPAN)], 2, below),
        shift(cnt_in.at[pl.ds(nb - SPAN, SPAN)], cnt.at[pl.ds(0, SPAN)], 3, above),
    ]
    xe[halo : halo + rows, :] = x_in[...]
    cnt[SPAN : SPAN + nb] = cnt_in[...]

    def project(e, c):
        at = pl.ds(pl.multiple_of(e * BS, BS), BS)
        _, normed = norm_rows(xe[at, :].astype(f32), gain_a[...])
        pair = matmul(normed, wqkv[:, d:])
        k, v = pair[:, :d].astype(bf), pair[:, d:].astype(bf)
        k_s[e], v_s[e] = k, v
        kt_s[e], vt_s[e] = k.T, v.T
        return c

    def project_q(b, c):
        at = pl.ds(pl.multiple_of((b + SPAN) * BS, BS), BS)
        _, normed = norm_rows(xe[at, :].astype(f32), gain_a[...])
        nrm_s[pl.ds(pl.multiple_of(b * BS, BS), BS), :] = normed
        q_s[b] = matmul(normed, wqkv[:, :d]).astype(bf)
        return c

    lax.fori_loop(SPAN, SPAN + nb, project, 0)
    lax.fori_loop(0, nb, project_q, 0)
    for copy in halos:
        copy.wait()
    lax.fori_loop(0, SPAN, project, 0)
    lax.fori_loop(nb + SPAN, ne, project, 0)

    def member(b, m):
        if m == 0:
            return b + SPAN
        return jnp.minimum(jnp.maximum(partners[b, m - 1] - first + SPAN, 0), ne - 1)

    def forward(b, c):
        for m in range(members):
            e = member(b, m)
            ksel[m * BS : (m + 1) * BS, :] = k_s[e]
            tsel[:, m * BS : (m + 1) * BS] = vt_s[e]
            slot = lax.broadcasted_iota(jnp.int32, (BS, BS), 0)
            limit = jnp.broadcast_to(cnt[e][:1, :], (BS, BS))
            bias[m * BS : (m + 1) * BS, :] = jnp.where(slot < limit, 0.0, -1e30)
        bd[0] = q_s[b].T

        def head(h, c):
            qm = jnp.where(head_mask((d, BS), 0, h), bd[0], 0)
            s = matmul(ksel[...], qm) + bias[...]
            top = jnp.max(s, axis=0, keepdims=True)
            e = jnp.exp((s - top) * scale)
            w = (e * (1.0 / jnp.sum(e, axis=0, keepdims=True))).astype(bf)
            lanes = pl.ds(pl.multiple_of(h * BS, BS), BS)
            wt[b, :, lanes] = w
            at = pl.ds(pl.multiple_of(h * HEAD, HEAD), HEAD)
            att_t[b, at, :] = matmul(tsel[at, :], w)
            return c

        lax.fori_loop(0, HEADS, head, 0)
        at = pl.ds(pl.multiple_of(b * BS, BS), BS)
        att = att_t[b].T.astype(bf)
        ga_s[at, :] = att
        mixed = x_in[at, :].astype(f32) + matmul(att, wout[...])
        mixed_s[at, :] = mixed
        nm_s[at, :] = norm_rows(mixed, gain_m[...])[1]
        return c

    lax.fori_loop(0, nb, forward, 0)

    acc1[...] = jnp.zeros_like(acc1)
    acc2[...] = jnp.zeros_like(acc2)
    step = 256
    for j in range(ff // step):
        lanes = slice(j * step, (j + 1) * step)
        up, down = wup[:, lanes], wdown[lanes, :]
        pre = matmul(nm_s[...], up)
        sq = pre * pre
        tangent = jnp.tanh(root_coef * (pre + 0.044715 * sq * pre))
        half = 0.5 * (1.0 + tangent)
        hidden = (pre * half).astype(bf)
        slope = half + 0.5 * pre * (1.0 - tangent * tangent) * root_coef * (
            1.0 + 3.0 * 0.044715 * sq
        )
        acc1[...] += matmul(hidden, down)
        src0[lanes, :] = outer_sum(hidden, cot[...]).astype(bf)
        grad_pre = (times_transpose(cot[...], down) * slope).astype(bf)
        src1[:, lanes] = outer_sum(nm_s[...], grad_pre).astype(bf)
        acc2[...] += times_transpose(grad_pre, up)

    def reduce_part(p, source, work, land, res):
        rest = stages[1:]
        turn = (2, 0, 1, 1)[p] % max(len(rest), 1)
        order = stages[:1] + rest[turn:] + rest[:turn]
        size, start, landing = source.shape[0], 0, 0
        history = []

        def remote(src, to, s, axis, partner):
            copy = pltpu.make_async_remote_copy(
                src_ref=src, dst_ref=to, send_sem=send.at[p, s], recv_sem=recv.at[p, s],
                device_id={axis: partner},
            )
            copy.start()
            return copy

        for s, (axis, bit) in enumerate(order):
            high, partner = flip(axis, bit)
            origin = source if s == 0 else work
            half = size // 2
            if half % 16 == 0:
                keep = pl.multiple_of(start + high * half, 16)
                give = pl.multiple_of(start + (1 - high) * half, 16)
                history.append((axis, partner, keep, half))
            else:
                half, keep, give = size, start, start
            copy = remote(
                origin.at[pl.ds(give, half)], land.at[pl.ds(landing, half)], s, axis, partner
            )
            yield
            copy.wait()
            here = origin[pl.ds(keep, half), :].astype(f32)
            there = land[landing : landing + half, :].astype(f32)
            target = res if s == count - 1 else work
            target[pl.ds(keep, half), :] = (here + there).astype(bf)
            start, size, landing = keep, half, landing + half
        for s, (axis, partner, keep, half) in enumerate(history[::-1]):
            region = res.at[pl.ds(keep, half)]
            copy = remote(region, region, count + s, axis, partner)
            yield
            copy.wait()
        (gdown_ref, gup_ref, gout_ref, gqkv_ref)[p][...] = res[...].astype(f32) * factor

    def reduce_gains():
        for s, (axis, bit) in enumerate(stages):
            copy = pltpu.make_async_remote_copy(
                src_ref=gwork.at[s], dst_ref=gainland.at[s], send_sem=send.at[4, s],
                recv_sem=recv.at[4, s], device_id={axis: flip(axis, bit)[1]},
            )
            copy.start()
            yield
            copy.wait()
            gwork[s + 1] = gwork[s] + gainland[s]
        ggain_a_ref[...] = gwork[count][0:1, :] * factor
        ggain_m_ref[...] = gwork[count][1:2, :] * factor

    running = [
        reduce_part(0, src0, work0, land0, res0),
        reduce_part(1, src1, work1, land1, res1),
    ]

    def advance():
        for part in list(running):
            if next(part, part) is part:
                running.remove(part)

    advance()

    mixed = mixed_s[...]
    out_ref[...] = (mixed + acc1[...]).astype(bf)
    inv = lax.rsqrt(jnp.mean(mixed * mixed, axis=-1, keepdims=True) + epsilon)
    through, gain_m_sum = norm_back(mixed, inv, gain_m[...], acc2[...])
    gmix = cot[...].astype(f32) + through
    acc1[...] = gmix
    gb = gmix.astype(bf)
    src2[...] = outer_sum(ga_s[...], gb).astype(bf)
    ga = times_transpose(gb, wout[...]).astype(bf)
    ga_s[...] = ga
    for b in range(nb):
        gat_s[b] = ga[b * BS : (b + 1) * BS, :].T
    gext[...] = jnp.zeros_like(gext)
    advance()
    running.append(reduce_part(2, src2, work2, land2, res2))
    next(running[-1])

    def spread(b, parts, lanes):
        gext[b + SPAN, :, lanes] += parts[0]
        for off in range(-SPAN, SPAN + 1):
            if off != 0:
                total = jnp.zeros_like(parts[0])
                for m in range(1, members):
                    hit = member(b, m) == b + SPAN + off
                    total = total + jnp.where(hit, parts[m], 0.0)
                gext[b + SPAN + off, :, lanes] += total

    for b in range(nb):
        for m in range(members):
            e = member(b, m)
            vsel[m * BS : (m + 1) * BS, :] = v_s[e]
            tsel[:, m * BS : (m + 1) * BS] = kt_s[e]

        def head(h, c):
            gm = jnp.where(head_mask((d, BS), 0, h), gat_s[b], 0)
            at = pl.ds(pl.multiple_of(h * HEAD, HEAD), HEAD)
            lanes = pl.ds(pl.multiple_of(h * BS, BS), BS)
            delta = jnp.sum(
                att_t[b, at, :] * gat_s[b, at, :].astype(f32), axis=0, keepdims=True
            )
            gw = matmul(vsel[...], gm)
            ds = (wt[b, :, lanes].astype(f32) * (gw - delta)).astype(bf)
            dst[:, lanes] = ds
            att_t[b, at, :] = matmul(tsel[at, :], ds) * scale
            return c

        lax.fori_loop(0, HEADS // 2, head, 0)
        advance()
        lax.fori_loop(HEADS // 2, HEADS, head, 0)
        advance()
        at = slice(b * BS, (b + 1) * BS)
        dq_s[at, :] = att_t[b].T.astype(bf)
        for h in range(HEADS):
            bd[h] = jnp.where(head_mask((BS, d), 1, h), q_s[b], 0)
        q_bd = bd[...].reshape(HEADS * BS, d)
        spread(
            b,
            [matmul(dst[m * BS : (m + 1) * BS, :], q_bd) * scale for m in range(members)],
            slice(0, d),
        )
        advance()
        for h in range(HEADS):
            bd[h] = jnp.where(head_mask((BS, d), 1, h), ga_s[at, :], 0)
        g_bd = bd[...].reshape(HEADS * BS, d)
        spread(
            b,
            [matmul(wt[b, m * BS : (m + 1) * BS, :], g_bd) for m in range(members)],
            slice(d, 2 * d),
        )
        advance()

    for i in range(SPAN):
        at = slice(i * BS, (i + 1) * BS)
        gsend[0, at, :] = gext[i].astype(bf)
        gsend[1, at, :] = gext[nb + SPAN + i].astype(bf)
    edges = [
        shift(gsend.at[0], gland.at[1], 4, below),
        shift(gsend.at[1], gland.at[0], 5, above),
    ]
    advance()
    for copy in edges:
        copy.wait()
    for i in range(SPAN):
        at = slice(i * BS, (i + 1) * BS)
        gext[SPAN + i] += gland[0, at, :].astype(f32)
        gext[nb + i] += gland[1, at, :].astype(f32)
    advance()
    pair = gext[SPAN : SPAN + nb].reshape(rows, 2 * d).astype(bf)
    packed = jnp.concatenate([dq_s[...], pair], axis=1)
    src3[...] = outer_sum(nrm_s[...], packed).astype(bf)
    running.insert(0, reduce_part(3, src3, work3, land3, res3))
    advance()
    row_values = x_in[...].astype(f32)
    inv = lax.rsqrt(jnp.mean(row_values * row_values, axis=-1, keepdims=True) + epsilon)
    back, gain_a_sum = norm_back(row_values, inv, gain_a[...], times_transpose(packed, wqkv[...]))
    pad = lax.broadcasted_iota(jnp.int32, (8, d), 0)
    gwork[0] = jnp.where(pad == 0, gain_a_sum[None, :], gain_m_sum[None, :])
    running.append(reduce_gains())
    advance()
    gvox_ref[...] = acc1[...] + back
    while running:
        advance()


def body(voxels, counts, partners, gain_attn, w_qkv, w_out, gain_mlp, w_up, w_down, cotangent):
    d = w_out.shape[0]
    nb = counts.shape[0]
    rows = voxels.shape[0]
    ne = nb + 2 * SPAN
    keys = (PART + 1) * BS
    ff = w_up.shape[1]
    bf, f32 = jnp.bfloat16, jnp.float32
    vmem = pl.BlockSpec(memory_space=pltpu.VMEM)
    smem = pl.BlockSpec(memory_space=pltpu.SMEM)
    shape = jax.ShapeDtypeStruct
    sizes = [(axis, lax.axis_size(axis)) for axis in ("space", "dp")]
    stages = stage_list(sizes)
    count = len(stages)
    parts = [(ff, d), (d, ff), (d, d), (d, 3 * d)]
    outs = pl.pallas_call(
        functools.partial(layer_kernel, stages, tuple(size for _, size in sizes)),
        out_shape=[
            shape((rows, d), bf),
            shape((rows, d), f32),
            shape((d, 3 * d), f32),
            shape((d, d), f32),
            shape((d, ff), f32),
            shape((ff, d), f32),
            shape((1, d), f32),
            shape((1, d), f32),
        ],
        in_specs=[vmem, vmem, smem] + [vmem] * 7,
        out_specs=[vmem] * 8,
        scratch_shapes=[
            pltpu.VMEM((ne * BS, d), bf),
            pltpu.VMEM((ne, 8, d), jnp.int32),
            pltpu.VMEM((rows, d), bf),
            pltpu.VMEM((ne, BS, d), bf),
            pltpu.VMEM((ne, BS, d), bf),
            pltpu.VMEM((ne, d, BS), bf),
            pltpu.VMEM((ne, d, BS), bf),
            pltpu.VMEM((nb, BS, d), bf),
            pltpu.VMEM((keys, d), bf),
            pltpu.VMEM((keys, d), bf),
            pltpu.VMEM((d, keys), bf),
            pltpu.VMEM((keys, BS), f32),
            pltpu.VMEM((nb, keys, HEADS * BS), bf),
            pltpu.VMEM((keys, HEADS * BS), bf),
            pltpu.VMEM((nb, d, BS), f32),
            pltpu.VMEM((nb, d, BS), bf),
            pltpu.VMEM((rows, d), bf),
            pltpu.VMEM((rows, d), f32),
            pltpu.VMEM((rows, d), bf),
            pltpu.VMEM((rows, d), f32),
            pltpu.VMEM((rows, d), f32),
            pltpu.VMEM((HEADS, BS, d), bf),
            pltpu.VMEM((rows, d), bf),
            pltpu.VMEM((ne, BS, 2 * d), f32),
            pltpu.VMEM((2, SPAN * BS, 2 * d), bf),
            pltpu.VMEM((2, SPAN * BS, 2 * d), bf),
        ]
        + [pltpu.VMEM(part, bf) for part in parts]
        + [pltpu.VMEM(part, bf) for part in parts]
        + [pltpu.VMEM((part[0] + 16 * count, part[1]), bf) for part in parts]
        + [pltpu.VMEM(part, bf) for part in parts]
        + [
            pltpu.VMEM((count + 1, 8, d), f32),
            pltpu.VMEM((count, 8, d), f32),
            pltpu.SemaphoreType.DMA((5, 2 * count)),
            pltpu.SemaphoreType.DMA((5, 2 * count)),
            pltpu.SemaphoreType.DMA((6,)),
            pltpu.SemaphoreType.DMA((6,)),
        ],
        compiler_params=pltpu.CompilerParams(
            collective_id=0, has_side_effects=True, vmem_limit_bytes=63 << 20
        ),
        name="layer",
    )(
        voxels, jnp.broadcast_to(counts[:, None, None], (nb, 8, d)), partners,
        gain_attn.reshape(1, d), w_qkv, w_out, gain_mlp.reshape(1, d), w_up, w_down, cotangent,
    )
    return (*outs[:6], outs[6].reshape(d), outs[7].reshape(d))


def solution(mesh):
    in_specs = (
        P(("dp", "space"), None),
        P(("dp", "space")),
        P(("dp", "space"), None),
        P(),
        P(),
        P(),
        P(),
        P(),
        P(),
        P(("dp", "space"), None),
    )
    out_specs = (P(("dp", "space"), None), P(("dp", "space"), None), P(), P(), P(), P(), P(), P())
    return jax.shard_map(body, mesh=mesh, in_specs=in_specs, out_specs=out_specs, check_vma=False)
```

```python
import functools
import math

import jax
import jax.numpy as jnp
from jax import lax
from jax.experimental import pallas as pl
from jax.experimental.pallas import tpu as pltpu
from jax.sharding import PartitionSpec as P

HEADS = 8
HEAD = 32
BS = 256
PART = 3
SPAN = 2


epsilon = 1e-06
root_coef = math.sqrt(2.0 / math.pi)


def matmul(left, right):
    return jnp.dot(left, right, preferred_element_type=jnp.float32)


def times_transpose(left, right):
    return lax.dot_general(
        left, right, (((1,), (1,)), ((), ())), preferred_element_type=jnp.float32
    )


def outer_sum(left, right):
    return lax.dot_general(
        left, right, (((0,), (0,)), ((), ())), preferred_element_type=jnp.float32
    )


def norm_rows(row_values, gain_vec):
    inv_rms = lax.rsqrt(jnp.mean(row_values * row_values, axis=-1, keepdims=True) + epsilon)
    return (inv_rms, (row_values * inv_rms * gain_vec).astype(jnp.bfloat16))


def norm_back(row_values, inv_rms, gain_vec, grad_norm):
    scaled_grad = grad_norm * gain_vec
    grad_rows = inv_rms * (
        scaled_grad
        - row_values
        * inv_rms
        * inv_rms
        * jnp.mean(scaled_grad * row_values, axis=-1, keepdims=True)
    )
    return (grad_rows, jnp.sum(grad_norm * row_values * inv_rms, axis=0))


def head_mask(shape, axis, head):
    return lax.broadcasted_iota(jnp.int32, shape, axis) // HEAD == head


def stage_list(sizes):
    stages = []
    for axis, size in sizes:
        bit = 1
        while bit < size:
            stages.append((axis, bit))
            bit *= 2
    return stages


def flip(axis, bit):
    me = lax.axis_index(axis)
    high = (me // bit) % 2
    return high, me + bit - 2 * bit * high


def layer_kernel(
    stages, sizes_sd, x_in, cnt_in, partners, gain_a, wqkv, wout, gain_m, wup, wdown, cot,
    out_ref, gvox_ref, gqkv_ref, gout_ref, gup_ref, gdown_ref, ggain_a_ref, ggain_m_ref,
    xe, cnt, nrm_s, k_s, v_s, kt_s, vt_s, q_s, ksel, vsel, tsel, bias, wt, dst, att_t, gat_s,
    ga_s, mixed_s, nm_s, acc1, acc2, bd, dq_s, gext, gsend, gland,
    src0, src1, src2, src3, work0, work1, work2, land0, land1, land2, land3,
    res3, gwork, gainland, send, recv, hsend, hrecv, tsend, trecv,
):
    d = wout.shape[0]
    rows = cot.shape[0]
    nb = rows // BS
    ne = nb + 2 * SPAN
    members = PART + 1
    ff = wup.shape[1]
    scale = 1.0 / math.sqrt(HEAD)
    bf, f32 = jnp.bfloat16, jnp.float32
    space, dp = sizes_sd
    me = lax.axis_index("space")
    first = (lax.axis_index("dp") * space + me) * nb
    below, above = (me + space - 1) % space, (me + 1) % space
    count = len(stages)
    halo = SPAN * BS
    factor = 1.0 / math.sqrt(rows * space * dp)

    barrier = pltpu.get_barrier_semaphore()
    groups = (("space", space), ("dp", dp))
    for axis, n in groups:
        for t in range(1, n):
            peer = (lax.axis_index(axis) + t) % n
            pl.semaphore_signal(barrier, inc=1, device_id={axis: peer})
    pl.semaphore_wait(barrier, space + dp - 2)

    def shift(src, dst, slot, target):
        copy = pltpu.make_async_remote_copy(
            src_ref=src, dst_ref=dst, send_sem=hsend.at[slot], recv_sem=hrecv.at[slot],
            device_id={"space": target},
        )
        copy.start()
        return copy

    halos = [
        shift(x_in.at[pl.ds(0, halo)], xe.at[pl.ds((nb + SPAN) * BS, halo)], 0, below),
        shift(x_in.at[pl.ds(rows - halo, halo)], xe.at[pl.ds(0, halo)], 1, above),
        shift(cnt_in.at[pl.ds(0, SPAN)], cnt.at[pl.ds(nb + SPAN, SPAN)], 2, below),
        shift(cnt_in.at[pl.ds(nb - SPAN, SPAN)], cnt.at[pl.ds(0, SPAN)], 3, above),
    ]
    xe[halo : halo + rows, :] = x_in[...]
    cnt[SPAN : SPAN + nb] = cnt_in[...]

    def project(e, c):
        at = pl.ds(pl.multiple_of(e * BS, BS), BS)
        _, normed = norm_rows(xe[at, :].astype(f32), gain_a[...])
        pair = matmul(normed, wqkv[:, d:])
        k, v = pair[:, :d].astype(bf), pair[:, d:].astype(bf)
        k_s[e], v_s[e] = k, v
        kt_s[e], vt_s[e] = k.T, v.T
        return c

    def project_q(b, c):
        at = pl.ds(pl.multiple_of((b + SPAN) * BS, BS), BS)
        _, normed = norm_rows(xe[at, :].astype(f32), gain_a[...])
        nrm_s[pl.ds(pl.multiple_of(b * BS, BS), BS), :] = normed
        q_s[b] = matmul(normed, wqkv[:, :d]).astype(bf)
        return c

    lax.fori_loop(SPAN, SPAN + nb, project, 0)
    lax.fori_loop(0, nb, project_q, 0)
    for copy in halos:
        copy.wait()
    lax.fori_loop(0, SPAN, project, 0)
    lax.fori_loop(nb + SPAN, ne, project, 0)

    def member(b, m):
        if m == 0:
            return b + SPAN
        return jnp.minimum(jnp.maximum(partners[b, m - 1] - first + SPAN, 0), ne - 1)

    def forward(b, c):
        for m in range(members):
            e = member(b, m)
            ksel[m * BS : (m + 1) * BS, :] = k_s[e]
            tsel[:, m * BS : (m + 1) * BS] = vt_s[e]
            slot = lax.broadcasted_iota(jnp.int32, (BS, BS), 0)
            limit = jnp.broadcast_to(cnt[e][:1, :], (BS, BS))
            bias[m * BS : (m + 1) * BS, :] = jnp.where(slot < limit, 0.0, -1e30)
        bd[0] = q_s[b].T

        def head(h, c):
            qm = jnp.where(head_mask((d, BS), 0, h), bd[0], 0)
            s = matmul(ksel[...], qm) + bias[...]
            top = jnp.max(s, axis=0, keepdims=True)
            e = jnp.exp((s - top) * scale)
            w = (e * (1.0 / jnp.sum(e, axis=0, keepdims=True))).astype(bf)
            lanes = pl.ds(pl.multiple_of(h * BS, BS), BS)
            wt[b, :, lanes] = w
            at = pl.ds(pl.multiple_of(h * HEAD, HEAD), HEAD)
            att_t[b, at, :] = matmul(tsel[at, :], w)
            return c

        lax.fori_loop(0, HEADS, head, 0)
        at = pl.ds(pl.multiple_of(b * BS, BS), BS)
        att = att_t[b].T.astype(bf)
        ga_s[at, :] = att
        mixed = x_in[at, :].astype(f32) + matmul(att, wout[...])
        mixed_s[at, :] = mixed
        nm_s[at, :] = norm_rows(mixed, gain_m[...])[1]
        return c

    lax.fori_loop(0, nb, forward, 0)

    acc1[...] = jnp.zeros_like(acc1)
    acc2[...] = jnp.zeros_like(acc2)
    step = 256
    for j in range(ff // step):
        lanes = slice(j * step, (j + 1) * step)
        up, down = wup[:, lanes], wdown[lanes, :]
        pre = matmul(nm_s[...], up)
        sq = pre * pre
        tangent = jnp.tanh(root_coef * (pre + 0.044715 * sq * pre))
        half = 0.5 * (1.0 + tangent)
        hidden = (pre * half).astype(bf)
        slope = half + 0.5 * pre * (1.0 - tangent * tangent) * root_coef * (
            1.0 + 3.0 * 0.044715 * sq
        )
        acc1[...] += matmul(hidden, down)
        src0[lanes, :] = outer_sum(hidden, cot[...]).astype(bf)
        grad_pre = (times_transpose(cot[...], down) * slope).astype(bf)
        src1[:, lanes] = outer_sum(nm_s[...], grad_pre).astype(bf)
        acc2[...] += times_transpose(grad_pre, up)

    def reduce_part(p, source, work, land, res):
        rest = stages[1:]
        turn = (2, 0, 1)[p] % max(len(rest), 1)
        order = stages[:1] + rest[turn:] + rest[:turn]
        size, start, landing = source.shape[0], 0, 0
        history = []

        def remote(src, to, s, axis, partner):
            copy = pltpu.make_async_remote_copy(
                src_ref=src, dst_ref=to, send_sem=send.at[p, s], recv_sem=recv.at[p, s],
                device_id={axis: partner},
            )
            copy.start()
            return copy

        for s, (axis, bit) in enumerate(order):
            high, partner = flip(axis, bit)
            origin = source if s == 0 else work
            half = size // 2
            if half % 16 == 0:
                keep = pl.multiple_of(start + high * half, 16)
                give = pl.multiple_of(start + (1 - high) * half, 16)
                history.append((axis, partner, keep, half))
            else:
                half, keep, give = size, start, start
            copy = remote(
                origin.at[pl.ds(give, half)], land.at[pl.ds(landing, half)], s, axis, partner
            )
            yield
            copy.wait()
            here = origin[pl.ds(keep, half), :].astype(f32)
            there = land[landing : landing + half, :].astype(f32)
            target = res if s == count - 1 else work
            target[pl.ds(keep, half), :] = (here + there).astype(bf)
            start, size, landing = keep, half, landing + half
        for s, (axis, partner, keep, half) in enumerate(history[::-1]):
            region = res.at[pl.ds(keep, half)]
            copy = remote(region, region, count + s, axis, partner)
            yield
            copy.wait()

    def to_group(pairs, slot, axis, n):
        copies = []
        for t in range(1, n):
            src, to = pairs(t, (lax.axis_index(axis) + t) % n)
            copy = pltpu.make_async_remote_copy(
                src_ref=src, dst_ref=to, send_sem=tsend.at[slot, t], recv_sem=trecv.at[slot, t],
                device_id={axis: (lax.axis_index(axis) + t) % n},
            )
            copy.start()
            copies.append(copy)
        return copies

    def reduce_wide():
        source, size, start, landing = src3, src3.shape[0], 0, 0
        history = []
        for s, (axis, n) in enumerate(groups):
            split = size % (16 * n) == 0
            piece = size // n if split else size
            here, base, origin = start, landing, source

            def outgoing(t, peer):
                give = pl.multiple_of(here + peer * piece, 16) if split else here
                to = land3.at[pl.ds(base + (t - 1) * piece, piece)]
                return origin.at[pl.ds(give, piece)], to

            copies = to_group(outgoing, s, axis, n)
            yield
            keep = pl.multiple_of(start + lax.axis_index(axis) * piece, 16) if split else start
            total = source[pl.ds(keep, piece), :].astype(f32)
            for t, copy in enumerate(copies):
                copy.wait()
                at = base + t * piece
                total = total + land3[at : at + piece, :].astype(f32)
            if split:
                history.append((axis, n, keep, piece))
            start, size, landing = keep, piece, landing + (n - 1) * piece
            source = res3.at[s]
            source[pl.ds(keep, piece), :] = total.astype(bf)
        final = res3.at[len(groups) - 1]
        for s, (axis, n, keep, piece) in enumerate(history[::-1]):
            region = final.at[pl.ds(keep, piece)]
            copies = to_group(lambda t, peer: (region, region), 2 + s, axis, n)
            yield
            for copy in copies:
                copy.wait()
        lanes = final.shape[1]
        for j in range(3 * d // lanes):
            gqkv_ref[:, j * lanes : (j + 1) * lanes] = final[j * d : (j + 1) * d, :]

    def reduce_gains():
        base = 0
        for s, (axis, n) in enumerate(groups):
            copies = to_group(
                lambda t, peer: (gwork.at[s], gainland.at[base + t - 1]), 4 + s, axis, n
            )
            yield
            total = gwork[s]
            for t, copy in enumerate(copies):
                copy.wait()
                total = total + gainland[base + t]
            gwork[s + 1] = total
            base += n - 1
        ggain_a_ref[...] = gwork[len(groups)][0:1, :] * factor
        ggain_m_ref[...] = gwork[len(groups)][1:2, :] * factor

    running = [
        reduce_part(0, src0, work0, land0, gdown_ref),
        reduce_part(1, src1, work1, land1, gup_ref),
    ]

    def advance():
        for part in list(running):
            if next(part, part) is part:
                running.remove(part)

    advance()

    mixed = mixed_s[...]
    out_ref[...] = (mixed + acc1[...]).astype(bf)
    inv = lax.rsqrt(jnp.mean(mixed * mixed, axis=-1, keepdims=True) + epsilon)
    through, gain_m_sum = norm_back(mixed, inv, gain_m[...], acc2[...])
    gmix = cot[...].astype(f32) + through
    acc1[...] = gmix
    gb = gmix.astype(bf)
    src2[...] = outer_sum(ga_s[...], gb).astype(bf)
    ga = times_transpose(gb, wout[...]).astype(bf)
    ga_s[...] = ga
    for b in range(nb):
        gat_s[b] = ga[b * BS : (b + 1) * BS, :].T
    gext[...] = jnp.zeros_like(gext)
    advance()
    running.append(reduce_part(2, src2, work2, land2, gout_ref))
    next(running[-1])

    def spread(b, parts, lanes):
        gext[b + SPAN, :, lanes] += parts[0]
        for off in range(-SPAN, SPAN + 1):
            if off != 0:
                total = jnp.zeros_like(parts[0])
                for m in range(1, members):
                    hit = member(b, m) == b + SPAN + off
                    total = total + jnp.where(hit, parts[m], 0.0)
                gext[b + SPAN + off, :, lanes] += total

    for b in range(nb):
        for m in range(members):
            e = member(b, m)
            vsel[m * BS : (m + 1) * BS, :] = v_s[e]
            tsel[:, m * BS : (m + 1) * BS] = kt_s[e]

        def head(h, c):
            gm = jnp.where(head_mask((d, BS), 0, h), gat_s[b], 0)
            at = pl.ds(pl.multiple_of(h * HEAD, HEAD), HEAD)
            lanes = pl.ds(pl.multiple_of(h * BS, BS), BS)
            delta = jnp.sum(
                att_t[b, at, :] * gat_s[b, at, :].astype(f32), axis=0, keepdims=True
            )
            gw = matmul(vsel[...], gm)
            ds = (wt[b, :, lanes].astype(f32) * (gw - delta)).astype(bf)
            dst[:, lanes] = ds
            att_t[b, at, :] = matmul(tsel[at, :], ds) * scale
            return c

        lax.fori_loop(0, HEADS // 2, head, 0)
        advance()
        lax.fori_loop(HEADS // 2, HEADS, head, 0)
        at = slice(b * BS, (b + 1) * BS)
        dq_s[at, :] = att_t[b].T.astype(bf)
        for h in range(HEADS):
            bd[h] = jnp.where(head_mask((BS, d), 1, h), q_s[b], 0)
        q_bd = bd[...].reshape(HEADS * BS, d)
        spread(
            b,
            [matmul(dst[m * BS : (m + 1) * BS, :], q_bd) * scale for m in range(members)],
            slice(0, d),
        )
        advance()
        for h in range(HEADS):
            bd[h] = jnp.where(head_mask((BS, d), 1, h), ga_s[at, :], 0)
        g_bd = bd[...].reshape(HEADS * BS, d)
        spread(
            b,
            [matmul(wt[b, m * BS : (m + 1) * BS, :], g_bd) for m in range(members)],
            slice(d, 2 * d),
        )

    for i in range(SPAN):
        at = slice(i * BS, (i + 1) * BS)
        gsend[0, at, :] = gext[i].astype(bf)
        gsend[1, at, :] = gext[nb + SPAN + i].astype(bf)
    edges = [
        shift(gsend.at[0], gland.at[1], 4, below),
        shift(gsend.at[1], gland.at[0], 5, above),
    ]
    for copy in edges:
        copy.wait()
    for i in range(SPAN):
        at = slice(i * BS, (i + 1) * BS)
        gext[SPAN + i] += gland[0, at, :].astype(f32)
        gext[nb + i] += gland[1, at, :].astype(f32)
    pair = gext[SPAN : SPAN + nb].reshape(rows, 2 * d).astype(bf)
    packed = jnp.concatenate([dq_s[...], pair], axis=1)
    qkv_sum = outer_sum(nrm_s[...], packed).astype(bf)
    lanes = src3.shape[1]
    for j in range(3 * d // lanes):
        src3[j * d : (j + 1) * d, :] = qkv_sum[:, j * lanes : (j + 1) * lanes]
    running.append(reduce_wide())
    next(running[-1])
    row_values = x_in[...].astype(f32)
    inv = lax.rsqrt(jnp.mean(row_values * row_values, axis=-1, keepdims=True) + epsilon)
    back, gain_a_sum = norm_back(row_values, inv, gain_a[...], times_transpose(packed, wqkv[...]))
    pad = lax.broadcasted_iota(jnp.int32, (8, d), 0)
    gwork[0] = jnp.where(pad == 0, gain_a_sum[None, :], gain_m_sum[None, :])
    running.append(reduce_gains())
    next(running[-1])
    gvox_ref[...] = acc1[...] + back
    while running:
        advance()


def body(voxels, counts, partners, gain_attn, w_qkv, w_out, gain_mlp, w_up, w_down, cotangent):
    d = w_out.shape[0]
    nb = counts.shape[0]
    rows = voxels.shape[0]
    ne = nb + 2 * SPAN
    keys = (PART + 1) * BS
    ff = w_up.shape[1]
    bf, f32 = jnp.bfloat16, jnp.float32
    vmem = pl.BlockSpec(memory_space=pltpu.VMEM)
    smem = pl.BlockSpec(memory_space=pltpu.SMEM)
    shape = jax.ShapeDtypeStruct
    sizes = [(axis, lax.axis_size(axis)) for axis in ("space", "dp")]
    stages = stage_list(sizes)
    count = len(stages)
    parts = [(ff, d), (d, ff), (d, d)]
    wide = (3 * d * d // 128, 128)
    outs = pl.pallas_call(
        functools.partial(layer_kernel, stages, tuple(size for _, size in sizes)),
        out_shape=[
            shape((rows, d), bf),
            shape((rows, d), f32),
            shape((d, 3 * d), bf),
            shape((d, d), bf),
            shape((d, ff), bf),
            shape((ff, d), bf),
            shape((1, d), f32),
            shape((1, d), f32),
        ],
        in_specs=[vmem, vmem, smem] + [vmem] * 7,
        out_specs=[vmem] * 8,
        scratch_shapes=[
            pltpu.VMEM((ne * BS, d), bf),
            pltpu.VMEM((ne, 8, d), jnp.int32),
            pltpu.VMEM((rows, d), bf),
            pltpu.VMEM((ne, BS, d), bf),
            pltpu.VMEM((ne, BS, d), bf),
            pltpu.VMEM((ne, d, BS), bf),
            pltpu.VMEM((ne, d, BS), bf),
            pltpu.VMEM((nb, BS, d), bf),
            pltpu.VMEM((keys, d), bf),
            pltpu.VMEM((keys, d), bf),
            pltpu.VMEM((d, keys), bf),
            pltpu.VMEM((keys, BS), f32),
            pltpu.VMEM((nb, keys, HEADS * BS), bf),
            pltpu.VMEM((keys, HEADS * BS), bf),
            pltpu.VMEM((nb, d, BS), f32),
            pltpu.VMEM((nb, d, BS), bf),
            pltpu.VMEM((rows, d), bf),
            pltpu.VMEM((rows, d), f32),
            pltpu.VMEM((rows, d), bf),
            pltpu.VMEM((rows, d), f32),
            pltpu.VMEM((rows, d), f32),
            pltpu.VMEM((HEADS, BS, d), bf),
            pltpu.VMEM((rows, d), bf),
            pltpu.VMEM((ne, BS, 2 * d), f32),
            pltpu.VMEM((2, SPAN * BS, 2 * d), bf),
            pltpu.VMEM((2, SPAN * BS, 2 * d), bf),
        ]
        + [pltpu.VMEM(part, bf) for part in parts + [wide]]
        + [pltpu.VMEM(part, bf) for part in parts]
        + [pltpu.VMEM((part[0] + 16 * count, part[1]), bf) for part in parts]
        + [
            pltpu.VMEM((2 * wide[0], wide[1]), bf),
            pltpu.VMEM((2,) + wide, bf),
            pltpu.VMEM((3, 8, d), f32),
            pltpu.VMEM((sum(size for _, size in sizes), 8, d), f32),
            pltpu.SemaphoreType.DMA((3, 2 * count)),
            pltpu.SemaphoreType.DMA((3, 2 * count)),
            pltpu.SemaphoreType.DMA((6,)),
            pltpu.SemaphoreType.DMA((6,)),
            pltpu.SemaphoreType.DMA((6, max(size for _, size in sizes))),
            pltpu.SemaphoreType.DMA((6, max(size for _, size in sizes))),
        ],
        compiler_params=pltpu.CompilerParams(
            collective_id=0, has_side_effects=True, vmem_limit_bytes=63 << 20
        ),
        name="layer",
    )(
        voxels, jnp.broadcast_to(counts[:, None, None], (nb, 8, d)), partners,
        gain_attn.reshape(1, d), w_qkv, w_out, gain_mlp.reshape(1, d), w_up, w_down, cotangent,
    )
    factor = 1.0 / math.sqrt(rows * sizes[0][1] * sizes[1][1])
    sums = [value.astype(f32) * factor for value in outs[2:6]]
    return (*outs[:2], *sums, outs[6].reshape(d), outs[7].reshape(d))


def solution(mesh):
    in_specs = (
        P(("dp", "space"), None),
        P(("dp", "space")),
        P(("dp", "space"), None),
        P(),
        P(),
        P(),
        P(),
        P(),
        P(),
        P(("dp", "space"), None),
    )
    out_specs = (P(("dp", "space"), None), P(("dp", "space"), None), P(), P(), P(), P(), P(), P())
    return jax.shard_map(body, mesh=mesh, in_specs=in_specs, out_specs=out_specs, check_vma=False)
```
